32 devices in a mesh: replica: 4 (over z), shard: 8 (over y, x, core).
Axes of the slice: x: 2, y: 2, z: 4, core: 2. Of those that a mesh axis runs over, the one named last changes fastest.
Arguments:
- tokens: bfloat16 [8192, 1024], P(('replica', 'shard')), may hold values from -64 to 64
- segment_ids: int32 [8192], P(('replica', 'shard')), may hold values from 0 to 93, as said below
- positions: int32 [8192], P(('replica', 'shard')), may hold values from 0 to 255, as said below
- w_qkv: bfloat16 [1024, 3072], P('shard'), may hold values from -2 to 2
- b_qkv: float32 [3072], P('shard'), may hold values from -3 to 3
- w_out: bfloat16 [1024, 1024], P('shard'), may hold values from -1 to 1
- b_out: float32 [1024], P('shard'), may hold values from -2 to 2
- w_up: bfloat16 [1024, 4096], P('shard'), may hold values from -0.1875 to 0.1875
- b_up: float32 [4096], P('shard'), may hold values from -3 to 3
- w_down: bfloat16 [4096, 1024], P('shard'), may hold values from -0.09375 to 0.09375
- b_down: float32 [1024], P('shard'), may hold values from -2 to 2
- gain_one: float32 [1024], P('shard'), may hold values from 0.25 to 1.75
- shift_one: float32 [1024], P('shard'), may hold values from -2 to 2
- gain_two: float32 [1024], P('shard'), may hold values from 0.25 to 1.75
- shift_two: float32 [1024], P('shard'), may hold values from -2 to 2
- cotangent: bfloat16 [8192, 1024], P(('replica', 'shard')), may hold values from -6 to 6
Outputs:
- block_out: bfloat16 [8192, 1024], P(('replica', 'shard'))
- d_tokens: bfloat16 [8192, 1024], P(('replica', 'shard'))
- d_w_qkv: float32 [1024, 3072], P('shard')
- d_b_qkv: float32 [3072], P('shard')
- d_w_out: float32 [1024, 1024], P('shard')
- d_b_out: float32 [1024], P('shard')
- d_w_up: float32 [1024, 4096], P('shard')
- d_b_up: float32 [4096], P('shard')
- d_w_down: float32 [4096, 1024], P('shard')
- d_b_down: float32 [1024], P('shard')
- d_gain_one: float32 [1024], P('shard')
- d_shift_one: float32 [1024], P('shard')
- d_gain_two: float32 [1024], P('shard')
- d_shift_two: float32 [1024], P('shard')
The draws below stay inside these ranges and needn't reach their ends.
Inputs may be any that keep to these rules, and one draw needn't show every extreme that they name: `segment_ids`: segment numbers never fall along the rows, start at 0, and a new segment begins at the first row of every sequence of 256 rows; the first sequence is one segment, and every later sequence holds exactly three segments. `positions`: A token's position is its distance from the first row of its segment.
All inputs are finite; a program needn't handle non-finite values.
Results may differ from the reference program's by a relative error of at most 0.015.
Values may be sent and summed in bfloat16 or wider, within the bound.
No kernel may reach another device: no remote copies, remote signals or barrier semaphores. Data moves between devices by JAX's collectives and lax.ppermute only.
A program may use at most 192 MiB of HBM per device.

```python
import jax
import jax.numpy as jnp
from jax import lax

D = 1024
H = 16
HD = 64
ROT = 16
FF = 4096
SEQ = 256
TOKENS = 8192


def segment_starts(key):
    token_index = jnp.arange(TOKENS, dtype=jnp.int32)
    blocks = TOKENS // SEQ
    within = token_index % SEQ
    seq_number = token_index // SEQ
    cut_first = jax.random.randint(jax.random.fold_in(key, 21), (blocks,), 1, SEQ // 2)
    cut_second = jax.random.randint(jax.random.fold_in(key, 22), (blocks,), SEQ // 2, SEQ)
    starts = (within == 0) | (within == cut_first[seq_number]) | (within == cut_second[seq_number])
    starts = jnp.where(token_index < SEQ, token_index == 0, starts)
    return (token_index, starts)


def draw_segment_ids(key, part):
    token_index, starts = segment_starts(key)
    return (jnp.cumsum(starts.astype(jnp.int32)) - 1).astype(jnp.int32)


def draw_positions(key, part):
    token_index, starts = segment_starts(key)
    begin_at = lax.cummax(jnp.where(starts, token_index, 0), axis=0)
    return (token_index - begin_at).astype(jnp.int32)


def draw_tokens(key, part):
    values = jax.random.normal(key, (TOKENS, D), jnp.float32)
    return jnp.clip(values, -6.0, 6.0).astype(jnp.bfloat16)


def draw_w_qkv(key, part):
    spread = D ** (-0.5)
    values = jnp.clip(jax.random.normal(key, (D, 3 * D), jnp.float32) * spread, -6.0 * spread, 6.0 * spread)
    return values.astype(jnp.bfloat16)


def levels(own_key, extent, split, smallest, top_value):
    def one(position, parts):
        draws = jax.random.uniform(jax.random.fold_in(jax.random.fold_in(own_key, 6), position), (parts,), jnp.float32, smallest / len(split), top_value / len(split))
        return jnp.repeat(jnp.exp(draws), extent[position] // parts).reshape((-1,) + (1,) * (len(extent) - position - 1))

    gain = one(*split[0])
    for cut in split[1:]:
        gain = gain * one(*cut)
    return gain


def noise(key, dims, deviation, limit, shards=(), held_as=jnp.bfloat16):
    entries = jax.random.normal(key, dims, jnp.float32) * deviation
    if len(shards) > 0:
        entries = levels(key, dims, shards, -0.22, 0.18) * entries
    return jnp.clip(entries, min=-limit, max=limit).astype(held_as)


def setup_inputs(seed: int = 0) -> dict:
    streams_of = jax.random.split(jax.random.key(seed), 17)
    tokens = draw_tokens(jax.random.fold_in(streams_of[16], 71), 0)
    segment_ids = draw_segment_ids(jax.random.fold_in(streams_of[16], 71), 0)
    positions = draw_positions(jax.random.fold_in(streams_of[16], 71), 0)
    w_qkv = draw_w_qkv(jax.random.fold_in(streams_of[16], 71), 0)
    b_qkv = noise(streams_of[4], (3 * D,), 0.5, 3.0, ((0, 8),), jnp.float32)
    w_out = noise(streams_of[5], (D, D), (D // 32) ** -0.5, 1.0, ((0, 8),))
    b_out = noise(streams_of[6], (D,), 0.3, 2.0, ((0, 8),), jnp.float32)
    w_up = noise(streams_of[7], (D, FF), D ** -0.5, 0.1875, ((0, 8),))
    b_up = noise(streams_of[8], (FF,), 0.5, 3.0, ((0, 8),), jnp.float32)
    w_down = noise(streams_of[9], (FF, D), FF ** -0.5, 0.09375, ((0, 8),))
    b_down = noise(streams_of[10], (D,), 0.3, 2.0, ((0, 8),), jnp.float32)
    gain_one = jnp.clip(1.0 + 0.15 * jax.random.normal(streams_of[11], (D,), jnp.float32), 0.25, 1.75)
    shift_one = noise(streams_of[12], (D,), 0.3, 2.0, ((0, 8),), jnp.float32)
    gain_two = jnp.clip(1.0 + 0.15 * jax.random.normal(streams_of[13], (D,), jnp.float32), 0.25, 1.75)
    shift_two = noise(streams_of[14], (D,), 0.3, 2.0, ((0, 8),), jnp.float32)
    cotangent = noise(streams_of[15], (TOKENS, D), 1.0, 6.0, ((0, 32),))
    return {"tokens": tokens, "segment_ids": segment_ids, "positions": positions, "w_qkv": w_qkv, "b_qkv": b_qkv, "w_out": w_out, "b_out": b_out, "w_up": w_up, "b_up": b_up, "w_down": w_down, "b_down": b_down, "gain_one": gain_one, "shift_one": shift_one, "gain_two": gain_two, "shift_two": shift_two, "cotangent": cotangent}


@jax.custom_vjp
def low(v):
    return lax.optimization_barrier(v.astype(jnp.bfloat16)).astype(jnp.float32)

@jax.custom_vjp
def low_back(v):
    return v

def low_keep(v):
    return (low(v), None)

def low_pass(kept, grad):
    return (grad,)

def back_keep(v):
    return (v, None)

def back_low(kept, grad):
    return (low(grad),)
low.defvjp(low_keep, low_pass)
low_back.defvjp(back_keep, back_low)
EPSILON = 1e-05
MASKED = -1e+30

def matmul_high(left, right):
    return jnp.dot(left, right, precision=lax.Precision.HIGHEST, preferred_element_type=jnp.float32)

def exact_gelu(values):
    return jax.nn.gelu(values, approximate=False)

def layer_norm(inputs, norm_gain, norm_shift):
    row_mean = lax.optimization_barrier(jnp.mean(inputs, axis=-1, keepdims=True))
    centred = inputs - row_mean
    variance = lax.optimization_barrier(jnp.mean(centred * centred, axis=-1, keepdims=True))
    return centred * lax.rsqrt(variance + EPSILON) * norm_gain + norm_shift

def rotary_tables(positions, rot_dims):
    half_rot = rot_dims // 2
    inverse_freq = 10000.0 ** (-jnp.arange(half_rot, dtype=jnp.float32) * 2.0 / rot_dims)
    angles = positions.astype(jnp.float32)[:, None] * inverse_freq[None, :]
    return (jnp.cos(angles)[:, None, :], jnp.sin(angles)[:, None, :])

def rotate(head_vals, cosine, sine_part, rot_dims):
    half_rot = rot_dims // 2
    leading = head_vals[..., :half_rot]
    trailing = head_vals[..., half_rot:rot_dims]
    passed = head_vals[..., rot_dims:]
    return jnp.concatenate([leading * cosine - trailing * sine_part, trailing * cosine + leading * sine_part, passed], axis=-1)

def forward_block(block_tokens, block_segments, cosine, sine_part, params):
    w_qkv, b_qkv, w_out, b_out, w_up, b_up, w_down, b_down, gain_one, shift_one, gain_two, shift_two = params
    seq_len = block_tokens.shape[0]
    normed_one = low(layer_norm(block_tokens, gain_one, shift_one))
    normed_two = low(layer_norm(block_tokens, gain_two, shift_two))
    projected = low_back(matmul_high(normed_one, w_qkv) + b_qkv).reshape(seq_len, 3, H, HD)
    queries = low(rotate(projected[:, 0], cosine, sine_part, ROT))
    key_rot = low(rotate(projected[:, 1], cosine, sine_part, ROT))
    value_low = low(projected[:, 2])
    raw_scores = jnp.einsum('qhd,khd->hqk', queries, key_rot, precision=lax.Precision.HIGHEST)
    scores = low_back(raw_scores * HD ** (-0.5))
    token_index = jnp.arange(seq_len)
    allowed = (block_segments[:, None] == block_segments[None, :]) & (token_index[None, :] <= token_index[:, None])
    scores = jnp.where(allowed[None], scores, MASKED)
    probs = low(jax.nn.softmax(scores, axis=-1))
    attended = jnp.einsum('hqk,khd->qhd', probs, value_low, precision=lax.Precision.HIGHEST).reshape(seq_len, H * HD)
    attended = low(low_back(attended))
    upper = low_back(matmul_high(normed_two, w_up) + b_up)
    hidden = low(exact_gelu(upper))
    return block_tokens + matmul_high(attended, w_out) + b_out + matmul_high(hidden, w_down) + b_down

def reference(tokens, segment_ids, positions, w_qkv, b_qkv, w_out, b_out, w_up, b_up, w_down, b_down, gain_one, shift_one, gain_two, shift_two, cotangent):
    params = tuple((member.astype(jnp.float32) for member in (w_qkv, b_qkv, w_out, b_out, w_up, b_up, w_down, b_down, gain_one, shift_one, gain_two, shift_two)))
    blocks = TOKENS // SEQ
    tok_blocks = tokens.astype(jnp.float32).reshape(blocks, SEQ, D)
    seg_blocks = segment_ids.reshape(blocks, SEQ)
    pos_blocks = positions.reshape(blocks, SEQ)
    cot_blocks = cotangent.astype(jnp.float32).reshape(blocks, SEQ, D)

    def one_block(totals, inputs):
        block_tokens, block_segments, block_positions, block_cot = inputs
        cosine, sine_part = rotary_tables(block_positions, ROT)

        def forward_fn(block_in, *param_list):
            return forward_block(block_in, block_segments, cosine, sine_part, param_list)
        result, pullback = jax.vjp(forward_fn, block_tokens, *params)
        grads = pullback(block_cot)
        new_totals = tuple((total + (low(grad) if member in (0, 2, 4, 6) else grad) for member, (total, grad) in enumerate(zip(totals, grads[1:]))))
        return (new_totals, (result.astype(jnp.bfloat16), grads[0].astype(jnp.bfloat16)))
    start_totals = tuple((jnp.zeros_like(member) for member in params))
    totals, (layer_outputs, input_grads) = lax.scan(one_block, start_totals, (tok_blocks, seg_blocks, pos_blocks, cot_blocks))
    grad_factor = TOKENS ** (-0.5)
    scaled = tuple((total * grad_factor for total in totals))
    return (layer_outputs.reshape(TOKENS, D), input_grads.reshape(TOKENS, D), scaled[0], scaled[1], scaled[2], scaled[3], scaled[4], scaled[5], scaled[6], scaled[7], scaled[8], scaled[9], scaled[10], scaled[11])
```

```python
import functools

import jax
import jax.numpy as jnp
import numpy as np
from jax import lax
from jax.experimental import pallas as pl
from jax.experimental.pallas import tpu as pltpu
from jax.sharding import PartitionSpec as P

H = 16
HD = 64
ROT = 16


EPSILON = 1e-05
MASKED = -1e30
CONTRACT_ROWS = (((0,), (0,)), ((), ()))
CONTRACT_COLS = (((1,), (1,)), ((), ()))


def exact_gelu(values):
    return jax.nn.gelu(values, approximate=False)


def rotary_tables(positions, rot_dims):
    half_rot = rot_dims // 2
    inverse_freq = 10000.0 ** (-jnp.arange(half_rot, dtype=jnp.float32) * 2.0 / rot_dims)
    angles = positions.astype(jnp.float32)[:, None] * inverse_freq[None, :]
    return (jnp.cos(angles)[:, None, :], jnp.sin(angles)[:, None, :])


def rotate(head_vals, cosine, sine_part, rot_dims):
    half_rot = rot_dims // 2
    leading = head_vals[..., :half_rot]
    trailing = head_vals[..., half_rot:rot_dims]
    passed = head_vals[..., rot_dims:]
    return jnp.concatenate(
        [leading * cosine - trailing * sine_part, trailing * cosine + leading * sine_part, passed],
        axis=-1,
    )


def masked_scores(queries, key_rot, allowed, score_scale):
    raw_scores = (
        jnp.einsum("qhd,khd->hqk", queries, key_rot, preferred_element_type=jnp.float32)
        * score_scale
    )
    return jnp.where(allowed[None], raw_scores, MASKED)


def gathered_body(
    tokens,
    segment_ids,
    positions,
    w_qkv,
    b_qkv,
    w_out,
    b_out,
    w_up,
    b_up,
    w_down,
    b_down,
    gain_one,
    shift_one,
    gain_two,
    shift_two,
    cotangent,
):
    seq_len, model_width = tokens.shape
    local_rows = w_qkv.shape[0]
    down_ratio = w_down.shape[0] // local_rows
    qkv_width = w_qkv.shape[1]
    score_scale = HD ** (-0.5)
    down_flat = w_down.reshape(local_rows, down_ratio * model_width)
    (
        bias_qkv,
        bias_out,
        bias_up,
        bias_down,
        complete_first_gain,
        full_shift_one,
        complete_second_gain,
        complete_second_shift,
    ) = (
        lax.all_gather(b_qkv, "shard", axis=0, tiled=True),
        lax.all_gather(b_out, "shard", axis=0, tiled=True),
        lax.all_gather(b_up, "shard", axis=0, tiled=True),
        lax.all_gather(b_down, "shard", axis=0, tiled=True),
        lax.all_gather(gain_one, "shard", axis=0, tiled=True),
        lax.all_gather(shift_one, "shard", axis=0, tiled=True),
        lax.all_gather(gain_two, "shard", axis=0, tiled=True),
        lax.all_gather(shift_two, "shard", axis=0, tiled=True),
    )
    inputs_f = tokens.astype(jnp.float32)
    row_mean = jnp.mean(inputs_f, axis=1, keepdims=True)
    centred = inputs_f - row_mean
    inv_std = lax.rsqrt(jnp.mean(centred * centred, axis=1, keepdims=True) + EPSILON)
    standardized_input = centred * inv_std
    normed_one = (standardized_input * complete_first_gain + full_shift_one).astype(jnp.bfloat16)
    normed_two = (standardized_input * complete_second_gain + complete_second_shift).astype(
        jnp.bfloat16
    )
    pieces = (
        lax.all_gather(w_qkv, "shard", axis=0, tiled=True),
        lax.all_gather(w_up, "shard", axis=0, tiled=True),
    )
    left_one = normed_one
    left_two = normed_two
    projected = jnp.dot(left_one, pieces[0], preferred_element_type=jnp.float32)
    upper = jnp.dot(left_two, pieces[1], preferred_element_type=jnp.float32)
    projected = projected + bias_qkv
    upper = upper + bias_up
    cosine, sine_part = rotary_tables(positions, ROT)
    split_heads = projected.reshape(seq_len, 3, H, HD)
    queries = rotate(split_heads[:, 0], cosine, sine_part, ROT).astype(jnp.bfloat16)
    key_rot = rotate(split_heads[:, 1], cosine, sine_part, ROT).astype(jnp.bfloat16)
    value_low = split_heads[:, 2].astype(jnp.bfloat16)
    token_index = jnp.arange(seq_len)
    allowed = (segment_ids[:, None] == segment_ids[None, :]) & (
        token_index[None, :] <= token_index[:, None]
    )
    scores = masked_scores(queries, key_rot, allowed, score_scale)
    row_max = jnp.max(scores, axis=2, keepdims=True)
    expo_vals = jnp.exp(scores - row_max)
    row_total = jnp.sum(expo_vals, axis=2, keepdims=True)
    log_total = row_max + jnp.log(row_total)
    probs_low = (expo_vals / row_total).astype(jnp.bfloat16)
    attended_low = (
        jnp.einsum("hqk,khd->qhd", probs_low, value_low, preferred_element_type=jnp.float32)
        .reshape(seq_len, model_width)
        .astype(jnp.bfloat16)
    )
    hidden_f, gelu_back = jax.vjp(exact_gelu, upper)
    hidden_low = hidden_f.astype(jnp.bfloat16)
    pieces = (
        lax.all_gather(w_out, "shard", axis=0, tiled=True),
        lax.all_gather(down_flat, "shard", axis=0, tiled=True),
    )
    piece_rows = pieces[0].shape[0]
    left_att = attended_low
    left_hid = hidden_low
    branches = jnp.dot(left_att, pieces[0], preferred_element_type=jnp.float32) + jnp.dot(
        left_hid,
        pieces[1].reshape(piece_rows * down_ratio, model_width),
        preferred_element_type=jnp.float32,
    )
    block_out = (inputs_f + branches + bias_out + bias_down).astype(jnp.bfloat16)
    cot_f = cotangent.astype(jnp.float32)
    pieces = (
        lax.all_gather(w_out, "shard", axis=0, tiled=True),
        lax.all_gather(down_flat, "shard", axis=0, tiled=True),
    )
    piece_rows = pieces[0].shape[0]
    part_att = lax.dot_general(
        cotangent, pieces[0], CONTRACT_COLS, preferred_element_type=jnp.float32
    )
    part_hid = lax.dot_general(
        cotangent,
        pieces[1].reshape(piece_rows * down_ratio, model_width),
        CONTRACT_COLS,
        preferred_element_type=jnp.float32,
    )
    d_att_low = part_att.astype(jnp.bfloat16).reshape(seq_len, H, HD)
    scores_again = masked_scores(queries, key_rot, allowed, score_scale)
    probs = jnp.exp(scores_again - log_total)
    d_probs = jnp.einsum("qhd,khd->hqk", d_att_low, value_low, preferred_element_type=jnp.float32)
    d_values = jnp.einsum("hqk,qhd->khd", probs_low, d_att_low, preferred_element_type=jnp.float32)
    d_scores = (probs * (d_probs - jnp.sum(probs * d_probs, axis=2, keepdims=True))).astype(
        jnp.bfloat16
    )
    d_queries = (
        jnp.einsum("hqk,khd->qhd", d_scores, key_rot, preferred_element_type=jnp.float32)
        * score_scale
    )
    d_keys = (
        jnp.einsum("hqk,qhd->khd", d_scores, queries, preferred_element_type=jnp.float32)
        * score_scale
    )
    d_projected = (
        jnp.stack(
            [
                rotate(d_queries, cosine, -sine_part, ROT),
                rotate(d_keys, cosine, -sine_part, ROT),
                d_values,
            ],
            axis=1,
        )
        .reshape(seq_len, qkv_width)
        .astype(jnp.bfloat16)
    )
    (d_up_f,) = gelu_back(part_hid)
    d_upper = d_up_f.astype(jnp.bfloat16)
    pieces = (
        lax.all_gather(w_qkv, "shard", axis=0, tiled=True),
        lax.all_gather(w_up, "shard", axis=0, tiled=True),
    )
    first_portion = lax.dot_general(
        d_projected, pieces[0], CONTRACT_COLS, preferred_element_type=jnp.float32
    )
    second_portion = lax.dot_general(
        d_upper, pieces[1], CONTRACT_COLS, preferred_element_type=jnp.float32
    )
    normalized_gradient = (
        first_portion * complete_first_gain + second_portion * complete_second_gain
    )
    d_inputs = inv_std * (
        normalized_gradient
        - jnp.mean(normalized_gradient, axis=1, keepdims=True)
        - standardized_input
        * jnp.mean(normalized_gradient * standardized_input, axis=1, keepdims=True)
    )
    d_tokens = (cot_f + d_inputs).astype(jnp.bfloat16)
    left_one = normed_one
    left_two = normed_two
    term_qkv = lax.dot_general(
        left_one, d_projected, CONTRACT_ROWS, preferred_element_type=jnp.float32
    )
    term_up = lax.dot_general(left_two, d_upper, CONTRACT_ROWS, preferred_element_type=jnp.float32)
    grad_in = lax.psum_scatter(
        jnp.concatenate([term_qkv, term_up], axis=1).astype(jnp.bfloat16),
        "shard",
        scatter_dimension=0,
        tiled=True,
    )
    left_att = attended_low
    left_hid = hidden_low
    term_att = lax.dot_general(
        left_att, cotangent, CONTRACT_ROWS, preferred_element_type=jnp.float32
    )
    term_hid = lax.dot_general(
        left_hid, cotangent, CONTRACT_ROWS, preferred_element_type=jnp.float32
    ).reshape(local_rows * lax.axis_size("shard"), down_ratio * model_width)
    grad_out = lax.psum_scatter(
        jnp.concatenate([term_att, term_hid], axis=1).astype(jnp.bfloat16),
        "shard",
        scatter_dimension=0,
        tiled=True,
    )
    sum_qkv = jnp.sum(d_projected, axis=0, dtype=jnp.float32)
    sum_cot = jnp.sum(cot_f, axis=0)
    sum_up = jnp.sum(d_upper, axis=0, dtype=jnp.float32)
    sum_gain_one = jnp.sum(first_portion * standardized_input, axis=0)
    sum_shift_one = jnp.sum(first_portion, axis=0)
    sum_gain_two = jnp.sum(second_portion * standardized_input, axis=0)
    sum_shift_two = jnp.sum(second_portion, axis=0)
    part_qkv, part_cot, part_up, part_gain_one, part_shift_one, part_gain_two, part_shift_two = (
        lax.psum_scatter(
            sum_qkv.astype(jnp.bfloat16), "shard", scatter_dimension=0, tiled=True
        ).astype(jnp.float32),
        lax.psum_scatter(
            sum_cot.astype(jnp.bfloat16), "shard", scatter_dimension=0, tiled=True
        ).astype(jnp.float32),
        lax.psum_scatter(
            sum_up.astype(jnp.bfloat16), "shard", scatter_dimension=0, tiled=True
        ).astype(jnp.float32),
        lax.psum_scatter(
            sum_gain_one.astype(jnp.bfloat16), "shard", scatter_dimension=0, tiled=True
        ).astype(jnp.float32),
        lax.psum_scatter(
            sum_shift_one.astype(jnp.bfloat16), "shard", scatter_dimension=0, tiled=True
        ).astype(jnp.float32),
        lax.psum_scatter(
            sum_gain_two.astype(jnp.bfloat16), "shard", scatter_dimension=0, tiled=True
        ).astype(jnp.float32),
        lax.psum_scatter(
            sum_shift_two.astype(jnp.bfloat16), "shard", scatter_dimension=0, tiled=True
        ).astype(jnp.float32),
    )
    summed = (
        lax.psum(grad_in, "replica").astype(jnp.float32),
        lax.psum(grad_out, "replica").astype(jnp.float32),
        lax.psum(part_qkv.astype(jnp.bfloat16), "replica").astype(jnp.float32),
        lax.psum(part_cot.astype(jnp.bfloat16), "replica").astype(jnp.float32),
        lax.psum(part_up.astype(jnp.bfloat16), "replica").astype(jnp.float32),
        lax.psum(part_gain_one.astype(jnp.bfloat16), "replica").astype(jnp.float32),
        lax.psum(part_shift_one.astype(jnp.bfloat16), "replica").astype(jnp.float32),
        lax.psum(part_gain_two.astype(jnp.bfloat16), "replica").astype(jnp.float32),
        lax.psum(part_shift_two.astype(jnp.bfloat16), "replica").astype(jnp.float32),
    )
    total_tokens = seq_len * lax.axis_size("replica") * lax.axis_size("shard")
    grad_factor = total_tokens ** (-0.5)
    d_w_qkv = summed[0][:, :qkv_width] * grad_factor
    d_w_up = summed[0][:, qkv_width:] * grad_factor
    d_w_out = summed[1][:, :model_width] * grad_factor
    d_w_down = (
        summed[1][:, model_width:].reshape(local_rows * down_ratio, model_width) * grad_factor
    )
    d_b_qkv = summed[2] * grad_factor
    d_b_shared = summed[3] * grad_factor
    d_b_up = summed[4] * grad_factor
    return (
        block_out,
        d_tokens,
        d_w_qkv,
        d_b_qkv,
        d_w_out,
        d_b_shared,
        d_w_up,
        d_b_up,
        d_w_down,
        d_b_shared,
        summed[5] * grad_factor,
        summed[6] * grad_factor,
        summed[7] * grad_factor,
        summed[8] * grad_factor,
    )


WIDTH = 128
CORE, SIDE_X, SIDE_Y = 1, 2, 4
VMEM_BYTES = 60 * 1024 * 1024
VMEM = pl.BlockSpec(memory_space=pltpu.VMEM)
SMEM = pl.BlockSpec(memory_space=pltpu.SMEM)
ROW_DOT = (((1,), (0,)), ((), ()))


def splits(mesh):
    return mesh.shape["shard"] * WIDTH == H * HD and mesh.shape["replica"] == 4


def dot(left, right, dims=ROW_DOT):
    return lax.dot_general(left, right, dims, preferred_element_type=jnp.float32)


def aligned(index, step):
    return pl.ds(pl.multiple_of(index * step, step), step)


def rotary_constants(seq_len):
    half = ROT // 2
    freq = 10000.0 ** (-np.arange(half) * 2.0 / ROT)
    angles = np.arange(seq_len)[:, None] * freq[None, :]
    cosine = np.ones((seq_len, HD))
    sine = np.zeros((seq_len, HD))
    cosine[:, :half] = cosine[:, half:ROT] = np.cos(angles)
    sine[:, :half] = -np.sin(angles)
    sine[:, half:ROT] = np.sin(angles)
    table = np.concatenate([np.tile(cosine, (1, WIDTH // HD)), np.tile(sine, (1, WIDTH // HD))], 1)
    terms = []
    for _ in range(3):
        term = table.astype(jnp.bfloat16)
        terms.append(term)
        table = table - term.astype(np.float64)
    return np.stack(terms)


def standardize(block):
    mean = jnp.mean(block, axis=1, keepdims=True)
    centred = block - mean
    inv_std = lax.rsqrt(jnp.mean(centred * centred, axis=1, keepdims=True) + EPSILON)
    return centred * inv_std, inv_std


def pack_kernel(place, w_qkv, w_up, cot, extra, own, core, far_x, far_y, far_xy, cot_out):
    group, parity = place[0], place[1]
    model = w_qkv.shape[1] // 3
    units = own.shape[1] - 3 * WIDTH

    def piece(out, owner):
        for third in range(3):
            out[:, third * WIDTH : (third + 1) * WIDTH] = w_qkv[
                :, aligned(third * (model // WIDTH) + owner, WIDTH)
            ]
        out[:, 3 * WIDTH :] = w_up[:, aligned(owner, units)]

    piece(own, group)
    piece(core, group ^ CORE)
    piece(far_x, group ^ (SIDE_X + parity))
    piece(far_y, group ^ (SIDE_Y + parity))
    piece(far_xy, group ^ (SIDE_X + SIDE_Y + parity))
    seq_len = cot.shape[0]
    cot_out[:seq_len, :] = cot[...]
    vector = extra[1:2, :]
    high = vector.astype(jnp.bfloat16).astype(jnp.float32)
    line = lax.broadcasted_iota(jnp.int32, (16, model), 0)
    lines = jnp.where(
        line == 0,
        extra[0:1, :],
        jnp.where(line == 1, high, jnp.where(line == 2, vector - high, 0.0)),
    )
    cot_out[seq_len:, :] = lines.astype(jnp.bfloat16)


def place_rows(place, pieces, store):
    group, parity = place[0], place[1]
    offsets = [0, CORE]
    offsets += [side + parity for side in (SIDE_X, SIDE_Y, SIDE_X + SIDE_Y)]
    offsets += [side + 1 - parity for side in (SIDE_X, SIDE_Y, SIDE_X + SIDE_Y)]
    for offset, piece in zip(offsets, pieces):
        store(group ^ offset, piece)


def forward_kernel(*refs):
    place = refs[0]
    toks, cots, pieces = refs[1:9], refs[9:17], refs[17:25]
    w_down, b_up = refs[25:27]
    dwd_mine, dwd_other = refs[27:29]
    mups = refs[29:37]
    hidden, d_upper, vectors, d_bias_up, cot_sum = refs[37:42]
    tok_s, cot_all, normed_all, w_up, bias_s, grad_up, grad_down = refs[42:]
    step = pl.program_id(0)
    group, parity = place[0], place[1]
    seq_len, model = tok_s.shape
    units = w_up.shape[1]
    rows = model // 8

    @pl.when(step == 0)
    def _():
        def store(owner, piece):
            w_up[aligned(owner, rows), :] = piece[:, 3 * WIDTH :]

        place_rows(place, pieces, store)
        vectors[...] = jnp.zeros_like(vectors)
        for offset in range(8):
            owner = group ^ offset
            lines = cots[offset][seq_len:, :].astype(jnp.float32)
            values = lines[1:2] + lines[2:3]
            bias_s[:, aligned(owner, 3 * WIDTH)] = values[:, : 3 * WIDTH]
            for kind in range(5):
                vectors[kind : kind + 1, aligned(owner, rows)] = values[
                    :, (3 + kind) * WIDTH : (4 + kind) * WIDTH
                ]
        for third in range(3):
            vectors[5:6, third * WIDTH : (third + 1) * WIDTH] = bias_s[
                :, aligned(third * (model // WIDTH) + group, WIDTH)
            ]
        d_bias_up[...] = jnp.zeros_like(d_bias_up)
        cot_sum[...] = jnp.zeros_like(cot_sum)

    for offset in range(8):

        @pl.when(step == offset)
        def _():
            tok_s[...] = toks[offset][...]
            cot_all[offset * seq_len : (offset + 1) * seq_len, :] = cots[offset][:seq_len, :]

    here = aligned(step, seq_len)
    xhat, _ = standardize(tok_s[...].astype(jnp.float32))
    normed = (xhat * vectors[2:3, :] + vectors[3:4, :]).astype(jnp.bfloat16)
    normed_all[here, :] = normed
    cot = cot_all[here, :]
    upper = dot(normed, w_up[...]) + b_up[...]
    d_hidden = dot(cot, w_down[...], CONTRACT_COLS)
    half_cdf = 0.5 + 0.5 * lax.erf(upper * (0.5**0.5))
    hidden[here, :] = (upper * half_cdf).astype(jnp.bfloat16)
    density = jnp.exp(-0.5 * upper * upper) * ((2.0 * np.pi) ** -0.5)
    d_up = (d_hidden * (half_cdf + upper * density)).astype(jnp.bfloat16)
    d_upper[here, :] = d_up
    d_bias_up[...] += jnp.sum(d_up.astype(jnp.float32), axis=0, keepdims=True)
    cot_sum[...] += jnp.sum(cot.astype(jnp.float32), axis=0, keepdims=True)

    @pl.when(step == 7)
    def _():
        grad_down[...] = dot(hidden[...], cot_all[...], CONTRACT_ROWS)
        dwd_mine[...] = grad_down[aligned(parity, units // 2), :].astype(jnp.bfloat16)
        dwd_other[...] = grad_down[aligned(1 - parity, units // 2), :].astype(jnp.bfloat16)
        grad_up[...] = dot(normed_all[...], d_upper[...], CONTRACT_ROWS)
        for offset in range(8):
            mups[offset][...] = grad_up[aligned(group ^ offset, rows), :].astype(jnp.bfloat16)


def turn(values, cosine, sine):
    lane = lax.broadcasted_iota(jnp.int32, values.shape, 1) % HD
    half = ROT // 2
    swapped = jnp.where(
        lane < half, pltpu.roll(values, WIDTH - half, 1), pltpu.roll(values, half, 1)
    )
    return values * cosine + swapped * sine


def backward_kernel(*refs):
    place = refs[0]
    toks, cots, pieces = refs[1:9], refs[9:17], refs[17:25]
    w_out, w_down, hidden, d_upper, vectors, d_bias_up, cot_sum, tables = refs[25:33]
    sums_odd, sums_even = refs[33:35]
    mqs = refs[35:43]
    dwo_mine, dwo_other = refs[43:45]
    tok_s, cot_all, line_s, normed_all, att_all, d_proj_all, w_qkv, w_up, stats, bias_sum, grad = refs[45:]
    step = pl.program_id(0)
    group, parity = place[0], place[1]
    seq_len, model = tok_s.shape
    rows = model // 8
    scale = HD**-0.5

    @pl.when(step == 0)
    def _():
        def store(owner, piece):
            w_qkv[aligned(owner, rows), :] = piece[:, : 3 * WIDTH]
            w_up[aligned(owner, rows), :] = piece[:, 3 * WIDTH :]

        place_rows(place, pieces, store)
        stats[...] = jnp.zeros_like(stats)
        bias_sum[...] = jnp.zeros_like(bias_sum)

    order = [1, 3, 5, 7, 0, 2, 4, 6]
    for turn_of, offset in enumerate(order):

        @pl.when(step == turn_of)
        def _():
            tok_s[...] = toks[offset][...]
            cot_all[offset * seq_len : (offset + 1) * seq_len, :] = cots[offset][:seq_len, :]
            line_s[...] = cots[offset][seq_len:, :seq_len]

    which = jnp.where(step < 4, 2 * step + 1, 2 * (step - 4))
    here = aligned(which, seq_len)
    xhat, _ = standardize(tok_s[...].astype(jnp.float32))
    normed = (xhat * vectors[0:1, :] + vectors[1:2, :]).astype(jnp.bfloat16)
    normed_all[here, :] = normed
    cot = cot_all[here, :]
    projected = dot(normed, w_qkv[...]) + vectors[5:6, : 3 * WIDTH]
    line = lax.broadcasted_iota(jnp.int32, (16, seq_len), 0)
    ones = jnp.where(line == 0, 1.0, 0.0).astype(jnp.bfloat16)
    position = dot(line_s[...], ones, CONTRACT_ROWS).astype(jnp.int32)
    row = lax.broadcasted_iota(jnp.int32, (seq_len, seq_len), 0)
    col = lax.broadcasted_iota(jnp.int32, (seq_len, seq_len), 1)
    allowed = (col <= row) & (col >= row - position)
    chosen = (col == position).astype(jnp.float32).astype(jnp.bfloat16)
    angles = dot(chosen, tables[0]) + dot(chosen, tables[1]) + dot(chosen, tables[2])
    cosine, sine = angles[:, :WIDTH], angles[:, WIDTH:]
    queries = (turn(projected[:, :WIDTH], cosine, sine) * scale).astype(jnp.bfloat16)
    keys = turn(projected[:, WIDTH : 2 * WIDTH], cosine, sine).astype(jnp.bfloat16)
    values = projected[:, 2 * WIDTH :].astype(jnp.bfloat16)
    d_att = dot(cot, w_out[...], CONTRACT_COLS).astype(jnp.bfloat16)
    head = lax.broadcasted_iota(jnp.int32, (seq_len, WIDTH), 1) // HD
    attended = d_query = d_key = d_value = 0.0
    for which_head in range(WIDTH // HD):

        def only(array):
            return jnp.where(head == which_head, array, jnp.zeros_like(array))

        head_keys, head_d_att = only(keys), only(d_att)
        scores = jnp.where(allowed, dot(queries, head_keys, CONTRACT_COLS), MASKED)
        expo = jnp.exp(scores - jnp.max(scores, axis=1, keepdims=True))
        probs = expo * (1.0 / jnp.sum(expo, axis=1, keepdims=True))
        probs_low = probs.astype(jnp.bfloat16)
        attended += dot(probs_low, only(values))
        d_probs = dot(head_d_att, values, CONTRACT_COLS)
        d_value += dot(probs_low, head_d_att, CONTRACT_ROWS)
        inner = jnp.sum(probs * d_probs, axis=1, keepdims=True)
        d_scores = (probs * (d_probs - inner)).astype(jnp.bfloat16)
        d_query += dot(d_scores, head_keys)
        d_key += dot(d_scores, only(queries), CONTRACT_ROWS)
    attended = attended.astype(jnp.bfloat16)
    att_all[here, :] = attended
    d_proj = jnp.concatenate(
        [turn(d_query * scale, cosine, -sine), turn(d_key, cosine, -sine), d_value], axis=1
    ).astype(jnp.bfloat16)
    d_proj_all[here, :] = d_proj
    bias_sum[...] += jnp.sum(d_proj.astype(jnp.float32), axis=0, keepdims=True)
    out = dot(attended, w_out[...]) + dot(hidden[here, :], w_down[...])
    first = dot(d_proj, w_qkv[...], CONTRACT_COLS)
    second = dot(d_upper[here, :], w_up[...], CONTRACT_COLS)
    stats[0:1, :] += jnp.sum(first * xhat, axis=0, keepdims=True)
    stats[1:2, :] += jnp.sum(first, axis=0, keepdims=True)
    stats[2:3, :] += jnp.sum(second * xhat, axis=0, keepdims=True)
    stats[3:4, :] += jnp.sum(second, axis=0, keepdims=True)
    low_out = out.astype(jnp.bfloat16)
    low_g = (first * vectors[0:1, :] + second * vectors[2:3, :]).astype(jnp.bfloat16)

    @pl.when(step < 4)
    def _():
        sums_odd[0, 0] = low_out
        sums_odd[0, 1] = low_g

    @pl.when(step >= 4)
    def _():
        sums_even[0, 0] = low_out
        sums_even[0, 1] = low_g

    @pl.when(step == 7)
    def _():
        grad_out = dot(att_all[...], cot_all[...], CONTRACT_ROWS)
        grad[:, : 3 * WIDTH] = dot(normed_all[...], d_proj_all[...], CONTRACT_ROWS)
        line16 = lax.broadcasted_iota(jnp.int32, (16, 3 * WIDTH), 0)
        for offset in range(8):
            owner = group ^ offset
            mq = mqs[offset]
            mq[:rows, :] = grad[aligned(owner, rows), : 3 * WIDTH].astype(jnp.bfloat16)
            four = [stats[kind : kind + 1, aligned(owner, rows)] for kind in range(4)]
            slots = []
            for block in range(3):
                number = 3 * owner + block
                third, slot_group = number // 8, number % 8
                piece = bias_sum[:, aligned(third, WIDTH)]
                slots.append(jnp.where(slot_group == group, piece, 0.0))
            first_line = jnp.concatenate(four[:3], axis=1)
            second_line = jnp.concatenate([four[3], jnp.zeros((1, 2 * WIDTH), jnp.float32)], axis=1)
            third_line = jnp.concatenate(slots, axis=1)
            lines = jnp.where(
                line16 == 0,
                first_line,
                jnp.where(line16 == 1, second_line, jnp.where(line16 == 2, third_line, 0.0)),
            )
            mq[rows:, :] = lines.astype(jnp.bfloat16)
        half = rows // 2
        grad[:rows, :] = grad_out
        units = d_bias_up.shape[1]
        line16 = lax.broadcasted_iota(jnp.int32, (16, model), 0)
        single = jnp.concatenate(
            [
                d_bias_up[...],
                cot_sum[:, aligned(group, rows)],
                jnp.zeros((1, model - units - rows), jnp.float32),
            ],
            axis=1,
        )
        lines = jnp.where(line16 == 0, single, 0.0).astype(jnp.bfloat16)
        dwo_mine[:half, :] = grad[aligned(parity, half), :].astype(jnp.bfloat16)
        dwo_mine[half:, :] = lines
        dwo_other[:half, :] = grad[aligned(1 - parity, half), :].astype(jnp.bfloat16)
        dwo_other[half:, :] = lines


def pick_kernel(place, *refs):
    blocks, mine, other = refs[:8], refs[8], refs[9]
    for parity in range(2):

        @pl.when(place[1] == parity)
        def _():
            for slot in range(4):
                mine[slot] = blocks[4 * parity + slot][...]
                other[slot] = blocks[4 * (1 - parity) + slot][...]


def finish_up_kernel(place, kept, received, out, *, factor):
    units = kept.shape[2]
    for slot in range(4):
        for side, blocks in ((place[1], kept), (1 - place[1], received)):
            sender = place[0] ^ (4 * side + slot)
            out[:, aligned(sender, units)] = blocks[slot].astype(jnp.float32) * factor


def finish_down_kernel(place, kept, received, out, *, factor):
    half = kept.shape[0]
    out[aligned(place[1], half), :] = kept[...].astype(jnp.float32) * factor
    out[aligned(1 - place[1], half), :] = received[...].astype(jnp.float32) * factor


def finish_qkv_kernel(
    place, kept, received, o_kept, o_received, out, d_out, d_b_qkv, g_one, s_one, g_two, s_two, d_b_up, d_b_out, d_b_down, *, factor
):
    rows = out.shape[0]
    model = out.shape[1] // 3
    lines = 0.0
    for slot in range(4):
        for side, blocks in ((place[1], kept), (1 - place[1], received)):
            sender = place[0] ^ (4 * side + slot)
            block = blocks[slot, :rows, :].astype(jnp.float32) * factor
            for third in range(3):
                out[:, aligned(third * (model // WIDTH) + sender, WIDTH)] = block[
                    :, third * WIDTH : (third + 1) * WIDTH
                ]
            lines += blocks[slot, rows:, :].astype(jnp.float32)
    lines = lines * factor
    g_one[...] = lines[0:1, :WIDTH]
    s_one[...] = lines[0:1, WIDTH : 2 * WIDTH]
    g_two[...] = lines[0:1, 2 * WIDTH :]
    s_two[...] = lines[1:2, :WIDTH]
    d_b_qkv[...] = lines[2:3, :]
    half = rows // 2
    d_out[aligned(place[1], half), :] = o_kept[:half, :].astype(jnp.float32) * factor
    d_out[aligned(1 - place[1], half), :] = o_received[:half, :].astype(jnp.float32) * factor
    single = o_kept[half:, :].astype(jnp.float32) * factor
    units = d_b_up.shape[1]
    d_b_up[...] = single[0:1, :units]
    d_b_out[...] = single[0:1, units : units + rows]
    d_b_down[...] = single[0:1, units : units + rows]


def token_kernel(tok, cot, vectors, own, from_x, from_y, block_out, d_tokens):
    total = (
        own[...].astype(jnp.float32)
        + from_x[...].astype(jnp.float32)
        + from_y[...].astype(jnp.float32)
    )
    inputs = tok[...].astype(jnp.float32)
    block_out[...] = (inputs + total[0] + vectors[4:5, :]).astype(jnp.bfloat16)
    xhat, inv_std = standardize(inputs)
    g = total[1]
    d_inputs = inv_std * (
        g
        - jnp.mean(g, axis=1, keepdims=True)
        - xhat * jnp.mean(g * xhat, axis=1, keepdims=True)
    )
    d_tokens[...] = (cot[...].astype(jnp.float32) + d_inputs).astype(jnp.bfloat16)


def call(kernel, args, outs, name, scratch=(), grid=None, out_specs=None):
    single = isinstance(outs, tuple)
    shapes = [outs] if single else outs
    shapes = [jax.ShapeDtypeStruct(*entry) for entry in shapes]
    specs = [SMEM if arg.ndim == 1 else VMEM for arg in args]
    if out_specs is None:
        out_specs = [VMEM] * len(shapes)
    extra = {} if grid is None else {"grid": grid}
    return pl.pallas_call(
        kernel,
        out_shape=shapes[0] if single else shapes,
        in_specs=specs,
        out_specs=out_specs[0] if single else out_specs,
        scratch_shapes=list(scratch),
        compiler_params=pltpu.CompilerParams(vmem_limit_bytes=VMEM_BYTES),
        name=name,
        **extra,
    )(*args)


def split_body(
    mesh,
    tokens,
    segment_ids,
    positions,
    w_qkv,
    b_qkv,
    w_out,
    b_out,
    w_up,
    b_up,
    w_down,
    b_down,
    gain_one,
    shift_one,
    gain_two,
    shift_two,
    cotangent,
):
    low = jnp.bfloat16
    seq_len, model = tokens.shape
    group_size, copies = mesh.shape["shard"], mesh.shape["replica"]
    rows = w_qkv.shape[0]
    units = w_down.shape[0]
    factor = (seq_len * group_size * copies) ** (-0.5)
    group = lax.axis_index("shard")
    parity = lax.axis_index("replica") % 2
    place = jnp.stack([group, parity]).astype(jnp.int32)

    def across(value, offset):
        return lax.ppermute(value, "shard", [(i, i ^ offset) for i in range(group_size)])

    def along(value, offset):
        return lax.ppermute(value, "replica", [(i, i ^ offset) for i in range(copies)])

    def crossed(value, side):
        pairs = [
            (z * group_size + i, z * group_size + (i ^ (side + z % 2)))
            for z in range(copies)
            for i in range(group_size)
        ]
        return lax.ppermute(value, ("replica", "shard"), pairs)

    def over_copies(mine, other):
        pair = mine + along(other, 1)
        total = pair + along(pair, 2)
        return total, along(total, 1)

    tok_x, tok_y = across(tokens, SIDE_X), across(tokens, SIDE_Y)
    vector = jnp.concatenate([b_qkv, gain_one, shift_one, gain_two, shift_two, b_out + b_down])
    place_line = jnp.pad(positions.astype(jnp.float32), (0, model - seq_len))
    extra = jnp.pad(jnp.stack([place_line, vector]), ((0, 6), (0, 0)))
    piece_shape = ((rows, 3 * WIDTH + units), low)
    own, core, far_x, far_y, far_xy, cot_own = call(
        pack_kernel,
        (place, w_qkv, w_up, cotangent, extra),
        [piece_shape] * 5 + [((seq_len + 16, model), low)],
        "pack",
    )
    w_x, w_y, w_xy = (
        crossed(far_x, SIDE_X),
        crossed(far_y, SIDE_Y),
        crossed(far_xy, SIDE_X + SIDE_Y),
    )
    w_core = across(core, CORE)
    cot_x, cot_y = across(cot_own, SIDE_X), across(cot_own, SIDE_Y)
    tok_xy, cot_xy = across(tok_y, SIDE_X), across(cot_x, SIDE_Y)
    pieces = (own, w_core, w_x, w_y, w_xy, along(w_x, 1), along(w_y, 1), along(w_xy, 1))
    toks, cots = [], []
    for tok, cot in ((tokens, cot_own), (tok_x, cot_x), (tok_y, cot_y), (tok_xy, cot_xy)):
        toks += [tok, across(tok, CORE)]
        cots += [cot, across(cot, CORE)]

    all_rows = seq_len * group_size
    outs = call(
        forward_kernel,
        (place, *toks, *cots, *pieces, w_down, b_up.reshape(1, units)),
        [((units // 2, model), low)] * 2
        + [((rows, units), low)] * 8
        + [((all_rows, units), low)] * 2
        + [((8, model), jnp.float32), ((1, units), jnp.float32), ((1, model), jnp.float32)],
        "forward",
        scratch=(
            pltpu.VMEM((seq_len, model), low),
            pltpu.VMEM((all_rows, model), low),
            pltpu.VMEM((all_rows, model), low),
            pltpu.VMEM((model, units), low),
            pltpu.VMEM((1, 3 * model), jnp.float32),
            pltpu.VMEM((model, units), jnp.float32),
            pltpu.VMEM((units, model), jnp.float32),
        ),
        grid=(8,),
    )
    down_kept, down_received = over_copies(outs[0], outs[1])
    mups = outs[2:10]
    hidden, d_upper, vectors, d_bias_up, cot_sum = outs[10:]
    mups = [mups[0]] + [across(mups[offset], offset) for offset in range(1, 8)]

    outs = call(
        backward_kernel,
        (
            place,
            *toks,
            *cots,
            *pieces,
            w_out,
            w_down,
            hidden,
            d_upper,
            vectors,
            d_bias_up,
            cot_sum,
            jnp.asarray(rotary_constants(seq_len)),
        ),
        [((4, 2, seq_len, model), low)] * 2
        + [((rows + 16, 3 * WIDTH), low)] * 8
        + [((rows // 2 + 16, model), low)] * 2,
        "backward",
        scratch=(
            pltpu.VMEM((seq_len, model), low),
            pltpu.VMEM((all_rows, model), low),
            pltpu.VMEM((16, seq_len), low),
            pltpu.VMEM((all_rows, model), low),
            pltpu.VMEM((all_rows, WIDTH), low),
            pltpu.VMEM((all_rows, 3 * WIDTH), low),
            pltpu.VMEM((model, 3 * WIDTH), low),
            pltpu.VMEM((model, units), low),
            pltpu.VMEM((8, model), jnp.float32),
            pltpu.VMEM((1, 3 * WIDTH), jnp.float32),
            pltpu.VMEM((model, model), jnp.float32),
        ),
        grid=(8,),
        out_specs=[
            pl.BlockSpec((1, 2, seq_len, model), lambda i: (jnp.minimum(i, 3), 0, 0, 0)),
            pl.BlockSpec((1, 2, seq_len, model), lambda i: (jnp.maximum(i - 4, 0), 0, 0, 0)),
        ]
        + [VMEM] * 10,
    )
    sums_odd, sums_even = outs[:2]
    mqs = outs[2:10]
    from_core = across(sums_odd, CORE)
    mqs = [mqs[0]] + [across(mqs[offset], offset) for offset in range(1, 8)]
    opposite = sums_even[3] + from_core[3]
    via_x, via_y = across(opposite[0], SIDE_X), across(opposite[1], SIDE_Y)
    sum_x = sums_even[1] + from_core[1]
    sum_y = sums_even[2] + from_core[2]
    sum_x = jnp.stack([sum_x[0], sum_x[1] + via_y])
    sum_y = jnp.stack([sum_y[0] + via_x, sum_y[1]])
    from_x, from_y = across(sum_x, SIDE_X), across(sum_y, SIDE_Y)
    own_sum = sums_even[0] + from_core[0]

    quarter = ((4, rows, units), low)
    up_kept, up_received = over_copies(*call(pick_kernel, (place, *mups), [quarter] * 2, "pick_up"))
    quarter = ((4, rows + 16, 3 * WIDTH), low)
    out_kept, out_received = over_copies(outs[10], outs[11])
    q_kept, q_received = over_copies(*call(pick_kernel, (place, *mqs), [quarter] * 2, "pick_qkv"))

    block_out, d_tokens = call(
        token_kernel,
        (tokens, cotangent, vectors, own_sum, from_x, from_y),
        [((seq_len, model), low)] * 2,
        "token",
    )
    d_w_down = call(
        functools.partial(finish_down_kernel, factor=factor),
        (place, down_kept, down_received),
        ((units, model), jnp.float32),
        "finish_down",
    )
    d_w_up = call(
        functools.partial(finish_up_kernel, factor=factor),
        (place, up_kept, up_received),
        ((rows, units * group_size), jnp.float32),
        "finish_up",
    )
    line = lambda size: ((1, size), jnp.float32)
    d_w_qkv, d_w_out, d_b_qkv, g_one, s_one, g_two, s_two, d_b_up, d_b_out, d_b_down = call(
        functools.partial(finish_qkv_kernel, factor=factor),
        (place, q_kept, q_received, out_kept, out_received),
        [
            ((rows, 3 * model), jnp.float32),
            ((rows, model), jnp.float32),
            line(3 * rows),
            line(rows),
            line(rows),
            line(rows),
            line(rows),
            line(units),
            line(rows),
            line(rows),
        ],
        "finish_qkv",
    )
    return (
        block_out,
        d_tokens,
        d_w_qkv,
        d_b_qkv.reshape(-1),
        d_w_out,
        d_b_out.reshape(-1),
        d_w_up,
        d_b_up.reshape(-1),
        d_w_down,
        d_b_down.reshape(-1),
        g_one.reshape(-1),
        s_one.reshape(-1),
        g_two.reshape(-1),
        s_two.reshape(-1),
    )


def solution(mesh):
    placed = (
        P(("replica", "shard"), None),
        P(("replica", "shard")),
        P(("replica", "shard")),
        P("shard", None),
        P("shard"),
        P("shard", None),
        P("shard"),
        P("shard", None),
        P("shard"),
        P("shard", None),
        P("shard"),
        P("shard"),
        P("shard"),
        P("shard"),
        P("shard"),
        P(("replica", "shard"), None),
    )
    return jax.shard_map(
        functools.partial(split_body, mesh) if splits(mesh) else gathered_body,
        mesh=mesh,
        in_specs=placed,
        out_specs=(
            P(("replica", "shard"), None),
            P(("replica", "shard"), None),
            P("shard", None),
            P("shard"),
            P("shard", None),
            P("shard"),
            P("shard", None),
            P("shard"),
            P("shard", None),
            P("shard"),
            P("shard"),
            P("shard"),
            P("shard"),
            P("shard"),
        ),
        check_vma=False,
    )
```
